32 devices in a mesh: rows: 8 (over z, core), cols: 4 (over y, x).
Axes of the slice: x: 2, y: 2, z: 4, core: 2. Of those that a mesh axis runs over, the one named last changes fastest.
Arguments:
- left_factor: float32 [2048, 2048], P('rows', 'cols'), may hold values from -0.125 to 0.125
- left_cot: float32 [2048, 2048], P('rows', 'cols'), may hold values from -6 to 6
- panel_factor: float32 [2, 256, 2048], P(None, 'cols', 'rows'), may hold values from -0.125 to 0.125
- panel_cot: float32 [2, 256, 2048], P(None, 'cols', 'rows'), may hold values from -6 to 6
- rows_factor: float32 [2, 256, 2048], P(None, 'rows', 'cols'), may hold values from -0.375 to 0.375
- rows_cot: float32 [2, 256, 2048], P(None, 'rows', 'cols'), may hold values from -6 to 6
- cross_factor: float32 [256, 256], P('cols', 'rows'), may hold values from -0.375 to 0.375
- cross_cot: float32 [256, 256], P('cols', 'rows'), may hold values from -6 to 6
- diag_factor: float32 [2, 256, 256], P(None, 'rows'), as said below
- diag_cot: float32 [2, 256, 256], P(None, 'rows'), may hold values from -6 to 6
Outputs:
- left_bar: float32 [2048, 2048], P('rows', 'cols')
- rows_bar: float32 [2, 256, 2048], P(None, 'rows', 'cols')
- panel_bar: float32 [2, 256, 2048], P(None, 'cols', 'rows')
- cross_bar: float32 [256, 256], P('cols', 'rows')
- diag_bar: float32 [2, 256, 256], P(None, 'rows')
The draws below stay inside these ranges and needn't reach their ends.
Inputs may be any that keep to these rules, and one draw needn't show every extreme that they name: `diag_factor`: each of the two blocks is lower triangular, with diagonal entries from 0.75 to 1.5; the entries below the diagonal are drawn independently with mean zero and spread at most 0.35 / sqrt(256), each of magnitude at most 1.4 / sqrt(256).
All inputs are finite; a program needn't handle non-finite values.
Results may differ from the reference program's by a relative error of at most 0.00016.
Values sent between devices are 32-bit elements; how exact they have to be, the bound alone decides.
No kernel may reach another device: no remote copies, remote signals or barrier semaphores. Data moves between devices by JAX's collectives and lax.ppermute only.
A program may use at most 64 MiB of HBM per device.

```python
import math
import jax
import jax.numpy as jnp
from jax import lax

NB = 256
M = 2048
K = 2048


def draw_diag_factor(key, part):
    first_key = jax.random.fold_in(key, 11)
    second_key = jax.random.fold_in(key, 12)
    lower = jnp.clip(jax.random.normal(first_key, (2, NB, NB), jnp.float32), -4.0, 4.0) * (0.35 / math.sqrt(NB))
    spread = jax.random.uniform(second_key, (2, NB), jnp.float32, 0.0, 1.0)
    leading = 0.75 * jnp.exp(spread * math.log(2.0))
    identity = jnp.eye(NB, dtype=jnp.float32)
    return jnp.tril(lower, -1) + leading[:, :, None] * identity[None, :, :]


def levels(own_key, shape, split, low, high):
    def one(dim, blocks):
        steps = jax.random.uniform(jax.random.fold_in(jax.random.fold_in(own_key, 6), dim), (blocks,), jnp.float32, low / len(split), high / len(split))
        return jnp.repeat(jnp.exp(steps), shape[dim] // blocks).reshape((-1,) + (1,) * (len(shape) - dim - 1))

    level = one(*split[0])
    for cut in split[1:]:
        level = level * one(*cut)
    return level


def bell_draw(key, extent, width, bound, split=(), kind=jnp.bfloat16):
    factor_of = levels(key, extent, split, -0.22, 0.18) if split else 1.0
    drawn = jax.random.normal(key, extent, jnp.float32) * width * factor_of
    return jnp.minimum(jnp.maximum(drawn, -bound), bound).astype(kind)


def setup_inputs(seed: int = 0) -> dict:
    key_of = jax.random.split(jax.random.key(seed), 11)
    left_factor = bell_draw(key_of[0], (M, K), M ** -0.5, 0.125, ((0, 8), (1, 4)), jnp.float32)
    left_cot = bell_draw(key_of[1], (M, K), 1.0, 6.0, ((0, 8), (1, 4)), jnp.float32)
    panel_factor = bell_draw(key_of[2], (2, NB, M), M ** -0.5, 0.125, ((1, 4), (2, 8)), jnp.float32)
    panel_cot = bell_draw(key_of[3], (2, NB, M), 1.0, 6.0, ((1, 4), (2, 8)), jnp.float32)
    rows_factor = bell_draw(key_of[4], (2, NB, K), NB ** -0.5, 0.375, ((1, 8), (2, 4)), jnp.float32)
    rows_cot = bell_draw(key_of[5], (2, NB, K), 1.0, 6.0, ((1, 8), (2, 4)), jnp.float32)
    cross_factor = bell_draw(key_of[6], (NB, NB), NB ** -0.5, 0.375, ((0, 4), (1, 8)), jnp.float32)
    cross_cot = bell_draw(key_of[7], (NB, NB), 1.0, 6.0, ((0, 4), (1, 8)), jnp.float32)
    diag_factor = draw_diag_factor(jax.random.fold_in(key_of[10], 71), 0)
    diag_cot = bell_draw(key_of[9], (2, NB, NB), 1.0, 6.0, ((1, 8),), jnp.float32)
    return {"left_factor": left_factor, "left_cot": left_cot, "panel_factor": panel_factor, "panel_cot": panel_cot, "rows_factor": rows_factor, "rows_cot": rows_cot, "cross_factor": cross_factor, "cross_cot": cross_cot, "diag_factor": diag_factor, "diag_cot": diag_cot}


highest = lax.Precision.HIGHEST

def product(former, latter):
    return jnp.dot(former.astype(jnp.float32), latter.astype(jnp.float32), precision=highest, preferred_element_type=jnp.float32)

def halved_lower(matrix):
    return jnp.tril(matrix) - 0.5 * jnp.diag(jnp.diag(matrix))

def solve_upper(factor, values):
    return lax.linalg.triangular_solve(factor, values, left_side=True, lower=True, transpose_a=True)

def reverse_block(factor, pending):
    shaped = halved_lower(product(factor.T, pending))
    middle = solve_upper(factor, shaped)
    transposed = solve_upper(factor, middle.T)
    return transposed + transposed.T

def reference(left_factor, left_cot, panel_factor, panel_cot, rows_factor, rows_cot, cross_factor, cross_cot, diag_factor, diag_cot):
    solved_two = solve_upper(diag_factor[1], panel_cot[1])
    left_next = left_cot - product(solved_two.T, rows_factor[1])
    first_cot = panel_cot[0] - product(cross_factor, solved_two)
    pending_two = diag_cot[1] - jnp.tril(product(solved_two, panel_factor[1].T))
    sym_two = reverse_block(diag_factor[1], pending_two)
    upper_rows = rows_cot[1] - product(solved_two, left_factor) - product(sym_two, rows_factor[1])
    cross_next = cross_cot - product(panel_factor[0], solved_two.T) - product(cross_factor, sym_two)
    solved_one = solve_upper(diag_factor[0], jnp.concatenate([cross_next, first_cot], axis=1))
    cross_part = solved_one[:, :NB]
    lower_part = solved_one[:, NB:]
    upper_rows = upper_rows - product(cross_part.T, rows_factor[0])
    left_next = left_next - product(lower_part.T, rows_factor[0])
    pending_one = diag_cot[0] - jnp.tril(product(cross_part, cross_factor.T) + product(lower_part, panel_factor[0].T))
    sym_one = reverse_block(diag_factor[0], pending_one)
    lower_rows = rows_cot[0] - product(cross_part, rows_factor[1]) - product(lower_part, left_factor) - product(sym_one, rows_factor[0])
    return (left_next, jnp.stack([lower_rows, upper_rows]), jnp.stack([lower_part, solved_two]), cross_part, jnp.stack([halved_lower(sym_one), halved_lower(sym_two)]))
```

```python
import functools
import jax
import jax.numpy as jnp
from jax import lax
from jax.experimental import pallas as pl
from jax.experimental.pallas import tpu as pltpu
from jax.sharding import PartitionSpec as P


f32, bf16 = jnp.float32, jnp.bfloat16


def exchange(value, axis, step):
    size = lax.axis_size(axis)
    return lax.ppermute(value, axis, [(i, i ^ step) for i in range(size)])


def ordered(pieces, index):
    pieces = list(pieces)
    step = 1
    while step < len(pieces):
        odd = (index // step) % 2 == 1
        for i in range(len(pieces)):
            if not i & step:
                low, high = pieces[i], pieces[i | step]
                pieces[i], pieces[i | step] = jnp.where(odd, high, low), jnp.where(odd, low, high)
        step *= 2
    return pieces


def gathered(value, axis, steps, index):
    return ordered([value] + [exchange(value, axis, step) for step in steps], index)


def split(value):
    high = value.astype(bf16)
    return high, (value - high.astype(f32)).astype(bf16)


def mul(a, b, dims=((1,), (0,))):
    (ah, al), (bh, bl) = a, b
    dot = functools.partial(lax.dot_general, dimension_numbers=(dims, ((), ())), preferred_element_type=f32)
    return dot(ah, bh) + (dot(ah, bl) + dot(al, bh))


def mm(a, b):
    return mul(split(a), split(b))


def iotas(n):
    return lax.broadcasted_iota(jnp.int32, (n, n), 0), lax.broadcasted_iota(jnp.int32, (n, n), 1)


def invert_kernel(factor_ref, out_ref):
    n = factor_ref.shape[0]
    rows, cols = iotas(n)
    factor = factor_ref[...]
    on_diag = rows == cols
    leading = jnp.sum(jnp.where(on_diag, factor, 0.0), axis=1, keepdims=True)
    scale = 1.0 / leading
    power = jnp.where(cols < rows, -factor * scale, 0.0)
    total = jnp.where(on_diag, 1.0, power)
    reach = 2
    while reach < n:
        parts = split(power)
        power = mul(parts, parts)
        total = total + mul(split(total), split(power))
        reach *= 2
    out_ref[...] = total.T * scale


def invert(factor):
    return pl.pallas_call(
        invert_kernel, out_shape=jax.ShapeDtypeStruct(factor.shape, f32), name="invert"
    )(factor)


def solve_kernel(inv_one_ref, inv_two_ref, cross_ref, cot_ref, left_ref, solved_ref, sums_ref):
    n = cross_ref.shape[0]
    two = mm(inv_two_ref[...], cot_ref[n:, :])
    solved_ref[n:, :] = two
    two = split(two)
    first = cot_ref[:n, :] - mul(split(cross_ref[...]), two)
    one = mm(inv_one_ref[...], first)
    solved_ref[:n, :] = one
    left = split(left_ref[...])
    sums_ref[n:, :] = mul(two, left)
    sums_ref[:n, :] = mul(split(one), left)


def small_kernel(d_ref, inv_ref, cross_ref, cross_cot_ref, dcot_ref, a_ref, b_ref, e_ref, sym_one_ref, sym_two_ref, bar_ref):
    n = cross_ref.shape[0]
    rows, cols = iotas(n)

    def phi(x):
        return jnp.where(rows > cols, x, jnp.where(rows == cols, 0.5 * x, 0.0))

    def tril(x):
        return jnp.where(rows >= cols, x, 0.0)

    def rev(factor, inv, pending):
        shaped = phi(mm(factor.T, pending))
        half = mm(inv, shaped)
        full = mul(split(half), split(inv), ((1,), (1,)))
        return full + full.T

    inv_one, inv_two = inv_ref[0], inv_ref[1]
    cross = split(cross_ref[...])
    part_two = mm(inv_two, a_ref[...])
    mixed = mm(inv_two, b_ref[...])
    sym_two = rev(d_ref[1], inv_two, dcot_ref[1] - tril(part_two))
    sym_two_ref[...] = sym_two
    own = mm(inv_one, e_ref[...] - mul(cross, split(mixed)))
    mid = cross_cot_ref[...] - mixed.T - mul(cross, split(sym_two))
    bar = mm(inv_one, mid)
    bar_ref[...] = bar
    pending = dcot_ref[0] - tril(mul(split(bar), cross, ((1,), (1,))) + own)
    sym_one_ref[...] = rev(d_ref[0], inv_one, pending)


def product(former, latter, dims=((1,), (0,))):
    return lax.dot_general(former, latter, (dims, ((), ())), precision=lax.Precision.HIGH, preferred_element_type=f32)


def on_device(left_factor, left_cot, panel_factor, panel_cot, rows_factor, rows_cot, cross_factor, cross_cot, diag_factor, diag_cot):
    n_rows, n_cols = lax.axis_size("rows"), lax.axis_size("cols")
    row, col = lax.axis_index("rows"), lax.axis_index("cols")
    n_far = n_rows // 2
    core, far = row % 2, row // 2
    first_core = core == 0
    n = diag_factor.shape[2]
    rs, cs = diag_factor.shape[1], panel_factor.shape[1]
    m, k = left_factor.shape
    assert cs == 2 * rs
    far_steps = [2 * i for i in range(1, n_far)]
    col_steps = list(range(1, n_cols))

    def mine(pair):
        return jnp.where(first_core, pair[0], pair[1])

    def theirs(pair):
        return jnp.where(first_core, pair[1], pair[0])

    def both(own, other, axis=0):
        return jnp.concatenate([jnp.where(first_core, own, other), jnp.where(first_core, other, own)], axis)

    def pair_up(own, other):
        return jnp.where(first_core, own, other), jnp.where(first_core, other, own)

    cots = gathered(panel_cot, "cols", col_steps, col)
    cot = jnp.concatenate([jnp.concatenate([o[p] for o in cots], 0) for p in range(2)], 0)

    dcot_cols = lax.dynamic_slice_in_dim(diag_cot, col * cs, cs, 2)
    diag_in = jnp.concatenate([diag_factor, dcot_cols], 2)
    diag_chip = both(mine(diag_in), exchange(theirs(diag_in), "rows", 1))
    bundle = jnp.concatenate([diag_chip, cross_factor, cross_cot], 1)
    far_all = jnp.concatenate(gathered(bundle, "rows", far_steps, far), 0)
    factor_own = far_all[:, :n]
    col_all = gathered(far_all[:, n:], "cols", col_steps, col)
    dcot_own = jnp.concatenate([o[:, :cs] for o in col_all], 1)

    def crossed(start):
        return jnp.concatenate(
            [jnp.concatenate([o[i * cs : (i + 1) * cs, start : start + rs] for i in range(n_far)], 1) for o in col_all], 0
        )

    packed = jnp.concatenate([factor_own, dcot_own, crossed(cs), crossed(cs + rs)], 1)
    other = exchange(packed, "rows", 1)
    low, high = pair_up(packed, other)
    factors = jnp.stack([low[:, :n], high[:, :n]])
    dcots = jnp.stack([low[:, n : 2 * n], high[:, n : 2 * n]])

    def interleave(start):
        return jnp.concatenate(
            [x[:, start + i * rs : start + (i + 1) * rs] for i in range(n_far) for x in (low, high)], 1
        )

    cross_whole = interleave(2 * n)
    cross_cot_whole = interleave(2 * n + n // 2)

    two_sum = product(cot[n:], panel_factor[1], ((1,), (1,)))
    one_sum = product(cot, panel_factor[0], ((1,), (1,)))
    sums = jnp.concatenate([two_sum, one_sum[n:], one_sum[:n]], 1)
    half = n // 2
    sums = lax.dynamic_slice_in_dim(sums, core * half, half, 0) + exchange(
        lax.dynamic_slice_in_dim(sums, (1 - core) * half, half, 0), "rows", 1
    )
    step = 2
    while step < n_rows:
        sums = sums + exchange(sums, "rows", step)
        step *= 2
    sums = jnp.concatenate(gathered(sums, "cols", col_steps, col), 1)
    sums = both(sums, exchange(sums, "rows", 1))

    def sum_of(which):
        return jnp.concatenate([sums[:, (3 * i + which) * cs : (3 * i + which + 1) * cs] for i in range(n_cols)], 1)

    inv_own = invert(factor_own)
    inv_one, inv_two = pair_up(inv_own, exchange(inv_own, "rows", 1))

    rows_own = both(mine(rows_factor), exchange(theirs(rows_factor), "rows", 1))
    rows_panel = jnp.concatenate(gathered(rows_own, "rows", far_steps, far), 0)
    rows_whole = both(rows_panel, exchange(rows_panel, "rows", 1))

    solved, local = pl.pallas_call(
        solve_kernel,
        out_shape=(jax.ShapeDtypeStruct((2 * n, m), f32), jax.ShapeDtypeStruct((2 * n, k), f32)),
        name="solve",
    )(inv_one, inv_two, cross_whole, cot, left_factor)

    local = local.reshape(2, n_far, 2, rs, k)
    local = local.transpose(2, 1, 0, 3, 4).reshape(2, n_far, 2 * rs, k)
    chip = mine(local) + exchange(theirs(local), "rows", 1)
    term = lax.dynamic_index_in_dim(chip, far, 0, False)
    for i in range(1, n_far):
        term = term + exchange(lax.dynamic_index_in_dim(chip, far ^ i, 0, False), "rows", 2 * i)

    sym_one, sym_two, bar = pl.pallas_call(
        small_kernel, out_shape=(jax.ShapeDtypeStruct((n, n), f32),) * 3, name="small"
    )(factors, jnp.stack([inv_one, inv_two]), cross_whole, cross_cot_whole, dcots, sum_of(0), sum_of(1), sum_of(2))

    left_bar = left_cot - product(solved, rows_whole, ((0,), (0,)))

    row_start = row * rs

    def own_rows(x):
        return lax.dynamic_slice_in_dim(x, row_start, rs, 0)

    sym_one_rows, sym_two_rows, bar_rows = own_rows(sym_one), own_rows(sym_two), own_rows(bar)
    bar_cols = lax.dynamic_slice_in_dim(bar, row_start, rs, 1)
    weights = jnp.concatenate(
        [jnp.concatenate([sym_one_rows, bar_rows], 1), jnp.concatenate([bar_cols.T, sym_two_rows], 1)], 0
    )
    rows_bar = rows_cot - (product(weights, rows_whole) + term).reshape(2, rs, k)

    panel_bar = lax.dynamic_slice_in_dim(solved.reshape(2, n, m), col * cs, cs, 1)
    cross_bar = lax.dynamic_slice_in_dim(bar_cols, col * cs, cs, 0)
    index = row_start + lax.broadcasted_iota(jnp.int32, (2, rs, n), 1)
    place = lax.broadcasted_iota(jnp.int32, (2, rs, n), 2)
    syms = jnp.stack([sym_one_rows, sym_two_rows])
    diag_bar = jnp.where(index > place, syms, jnp.where(index == place, 0.5 * syms, 0.0))
    return (left_bar, rows_bar, panel_bar, cross_bar, diag_bar)


def solution(mesh):
    whole, panel, across, square = P("rows", "cols"), P(None, "cols", "rows"), P(None, "rows", "cols"), P("cols", "rows")
    block = P(None, "rows", None)
    return jax.shard_map(
        on_device,
        mesh=mesh,
        in_specs=(whole, whole, panel, panel, across, across, square, square, block, block),
        out_specs=(whole, across, panel, square, block),
        check_vma=False,
    )
```
